32 devices in a mesh: expert: 8 (over z, y), tensor: 4 (over x, core).
Axes of the slice: x: 2, y: 2, z: 4, core: 2. Of those that a mesh axis runs over, the one named last changes fastest.
Arguments:
- attn_partial: bfloat16 [4, 2048, 7168], P('tensor', 'expert'), may hold values from -4 to 4
- residual: bfloat16 [2048, 7168], P(('expert', 'tensor')), may hold values from -6 to 6
- norm_gain: float32 [7168], replicated, may hold values from 0.25 to 1.75
- channel_order: int32 [7168], replicated, may hold values from 0 to 7167, each once
- rotation: bfloat16 [56, 128, 128], replicated, may hold values from -0.5 to 0.5
- routes: int32 [2048, 8], P(('expert', 'tensor')), may hold values from 0 to 31, all different within a row; in each aligned block of 64 rows (0 to 63, 64 to 127, ...) at most 24 rows name the same one
- slab_block: int32 [32], P(('expert', 'tensor')), may hold values from 0 to 52
Outputs:
- hessian: bfloat16 [32, 7168, 512], P(('expert', 'tensor'))
The draws below stay inside these ranges and needn't reach their ends.
Inputs may be any that keep to these rules, and one draw needn't show every extreme that they name: `routes`: tokens are numbered in the order of their devices along expert+tensor, 256 // 4 a device. Each token names 8 different experts; every expert is named by some token; the tokens of one device name one expert at most 24 times, and exactly 24 times somewhere.
All inputs are finite; a program needn't handle non-finite values.
Results may differ from the reference program's by a relative error of at most 0.018.
Values may be sent and summed in bfloat16 or wider, within the bound.
A program may use at most 128 MiB of HBM per device.

```python
import math
import jax
import jax.numpy as jnp
import numpy as np
from jax import lax

D = 7168
TOP = 8
BLK = 128
SLAB = 512
TOK_DEV = 256
EXPERTS = 32
TOKENS = 2048
CAP = 24
N_EXPERT = 8
N_TENSOR = 4


def with_ends(array, own_key, least, largest):
    longest = array.shape.index(max(array.shape))
    spots = []
    for shift in (0, 1):
        where = [jax.random.randint(jax.random.fold_in(own_key, axis), (), 0, length) for axis, length in enumerate(array.shape)]
        where[longest] = (where[longest] + shift) % array.shape[longest]
        spots.append(tuple(where))
    return array.at[spots[0]].set(least).at[spots[1]].set(largest)


def spiked(drawn, own_key, source, target, blocks, factor):
    def block_of(axis_at):
        return (jnp.arange(drawn.shape[axis_at]) // (drawn.shape[axis_at] // blocks)).reshape((-1,) + (1,) * (drawn.ndim - 1 - axis_at))

    first = jax.random.permutation(own_key, blocks)[block_of(target)]
    other_side = (block_of(target) + blocks // 2) % blocks
    return jnp.where((block_of(source) == first) | (block_of(source) == other_side), factor * drawn, drawn)


def block_scale(rng, extent, split, least, largest):
    gain = 1.0
    for axis_at, blocks in split:
        draws = jax.random.uniform(jax.random.fold_in(jax.random.fold_in(rng, 6), axis_at), (blocks,), jnp.float32, least / len(split), largest / len(split))
        gain = gain * jnp.repeat(jnp.exp(draws), extent[axis_at] // blocks).reshape((-1,) + (1,) * (len(extent) - 1 - axis_at))
    return gain


def routed_block(own_key, own, number, rows, number_of, top, reach, slope):
    ranking = jax.random.permutation(own_key, number_of)
    packed, ordinary = load_shares(number_of, rows * top, reach, slope, True), load_shares(number_of, rows * top, reach, slope, False)
    places = jnp.arange(number_of)

    def named(tallies, turn):
        used = int((tallies > 0).sum())
        fixed = max(1, used // 4)
        moved = fixed + (places - fixed + turn * (used - fixed)) % max(1, number_of - fixed)
        return jnp.zeros((number_of,), jnp.int32).at[ranking[jnp.where(places < fixed, places, moved)]].set(jnp.asarray(tallies, jnp.int32))

    tallies = jnp.where(number % 4 == 0, named(packed, number // 4), named(ordinary, number - number // 4 - 1))
    mixed = jax.random.permutation(jax.random.fold_in(own, 3), number_of)
    giver, sink = mixed[0:number_of // 2 * 2:2], mixed[1:number_of // 2 * 2:2]
    slack = jnp.minimum(tallies[giver] - 1, reach - tallies[sink]) // 2
    slack = jnp.where((giver == ranking[0]) | (sink == ranking[0]) | (tallies[sink] == 0), 0, jnp.maximum(slack, 0))
    moved = jax.random.randint(jax.random.fold_in(own, 4), (number_of // 2,), 0, 1 << 20) % (slack + 1)
    tallies = tallies.at[giver].add(-moved).at[sink].add(moved)
    items = jnp.searchsorted(jnp.cumsum(tallies), jnp.arange(rows * top), side="right").astype(jnp.int32)
    table = items.reshape(top, rows).T
    table = table[jax.random.permutation(jax.random.fold_in(own, 1), rows)]
    turn = jax.random.randint(jax.random.fold_in(own, 2), (rows, 1), 0, top)
    return jnp.take_along_axis(table, (jnp.arange(top)[None, :] + turn) % top, axis=1)


def load_shares(amount, total, most, slope, full):
    loads = [(1 << 20) // math.isqrt(grade ** slope) + 1 for grade in range(1, amount + 1)]
    largest = most if full else min(most, max(-(-total // amount), total * loads[0] // sum(loads)))
    least = 1 if total - largest >= amount - 1 else 0
    holding, rest = [largest] + [least] * (amount - 1), total - largest - least * (amount - 1)
    while rest > 0:
        free = [i for i in range(1, amount) if holding[i] < largest] or [i for i in range(1, amount) if holding[i] < most]
        pool, budget = sum([loads[i] for i in free]), rest
        for i in free:
            extra = min(most - holding[i], max(1, budget * loads[i] // pool), rest)
            holding[i] = holding[i] + extra
            rest = rest - extra
    return np.array(holding)


def centred(stream_key, shape, spread, bound, shards=(), kind=jnp.bfloat16):
    values = spread * jax.random.normal(stream_key, shape, jnp.float32)
    if shards:
        values = values * block_scale(stream_key, shape, shards, -0.22, 0.18)
    return jnp.clip(values, -bound, bound).astype(kind)


def bell_draw_with(stream_key, shape, width, reach, cuts, heavy, kind=jnp.bfloat16):
    drawn = width * jax.random.normal(stream_key, shape, jnp.float32)
    if cuts:
        drawn = drawn * block_scale(stream_key, shape, cuts, -0.22, 0.18)
    return jnp.clip(spiked(drawn, jax.random.fold_in(stream_key, 3), *heavy), -reach, reach).astype(kind)


def setup_inputs(seed: int = 0) -> dict:
    arg_keys = jax.random.split(jax.random.key(seed), 8)
    attn_partial = bell_draw_with(arg_keys[0], (N_TENSOR, TOKENS, D), 0.5, 4.0, ((0, 4), (1, 8)), (0, 1, 4, 2.0))
    residual = centred(arg_keys[1], (TOKENS, D), 1.0, 6.0, ((0, 32),))
    norm_gain = jnp.clip(1.0 + 0.15 * jax.random.normal(arg_keys[2], (D,), jnp.float32), 0.25, 1.75)
    channel_order = jax.random.permutation(arg_keys[3], D).astype(jnp.int32)
    rotation = centred(arg_keys[4], (D // BLK, BLK, BLK), BLK ** -0.5, 0.5)
    routes_keys = jax.random.split(jax.random.fold_in(arg_keys[5], 1), TOKENS // (TOK_DEV // N_TENSOR))
    routes_turns = jax.random.permutation(jax.random.fold_in(arg_keys[5], 3), TOKENS // (TOK_DEV // N_TENSOR))
    routes = jax.vmap(lambda own, number: routed_block(jax.random.fold_in(arg_keys[5], 2), own, number, TOK_DEV // N_TENSOR, EXPERTS, TOP, CAP, 2))(routes_keys, routes_turns).reshape((TOKENS, TOP))
    slab_block = with_ends(jax.random.randint(arg_keys[6], (EXPERTS,), 0, D // BLK - SLAB // BLK + 1), jax.random.fold_in(arg_keys[6], 1), 0, (D // BLK - SLAB // BLK + 1) - 1).astype(jnp.int32)
    return dict(attn_partial=attn_partial, residual=residual, norm_gain=norm_gain, channel_order=channel_order, rotation=rotation, routes=routes, slab_block=slab_block)


def rotate_rows(rows, channel_order, rotation):
    moved = jnp.take(rows, channel_order, axis=1)
    blocks = moved.reshape(rows.shape[0], rotation.shape[0], rotation.shape[1]).astype(jnp.float32)
    out = jnp.einsum('rbi,bij->rbj', blocks, rotation.astype(jnp.float32))
    return out.reshape(rows.shape[0], -1).astype(jnp.bfloat16)

def reference(attn_partial, residual, norm_gain, channel_order, rotation, routes, slab_block):
    attn = lax.optimization_barrier(jnp.sum(attn_partial.astype(jnp.float32), axis=0))
    hidden = residual.astype(jnp.float32) + attn
    scale = lax.rsqrt(lax.optimization_barrier(jnp.mean(hidden * hidden, axis=1, keepdims=True)) + 1e-06)
    normed = (hidden * scale * norm_gain[None, :]).astype(jnp.bfloat16)
    rotated = rotate_rows(normed, channel_order, rotation)
    limit = CAP * N_EXPERT * N_TENSOR
    expert_ids = jnp.arange(EXPERTS, dtype=jnp.int32)

    def one_expert(args):
        expert_id, block_id = args
        chosen = jnp.any(routes == expert_id, axis=1)
        keys = jnp.where(chosen, 0, 1).astype(jnp.int32)
        picked = jnp.argsort(keys, stable=True)[:limit].astype(jnp.int32)
        rows = rotated[picked] * chosen[picked][:, None].astype(jnp.bfloat16)
        count = jnp.sum(chosen.astype(jnp.float32))
        start = (block_id * BLK).astype(jnp.int32)
        slab = lax.dynamic_slice_in_dim(rows, start, SLAB, 1)
        product = lax.dot_general(rows, slab, (((0,), (0,)), ((), ())), preferred_element_type=jnp.float32)
        return (product * (2.0 / count)).astype(jnp.bfloat16)
    return lax.map(one_expert, (expert_ids, slab_block))
```

```python
import jax
import jax.numpy as jnp
from jax import lax
from jax.sharding import PartitionSpec as P

SLAB = 512


def rotate_rows(rows, channel_order, rotation):
    moved = jnp.take(rows, channel_order, axis=1)
    blocks = moved.reshape(rows.shape[0], rotation.shape[0], rotation.shape[1])
    out = jnp.einsum("rbi,bij->rbj", blocks, rotation, preferred_element_type=jnp.float32)
    return out.reshape(rows.shape[0], -1).astype(jnp.bfloat16)


def dispatch_rows(payload, routes):
    count_expert = lax.axis_size("expert")
    count_tensor = lax.axis_size("tensor")
    experts = count_expert * count_tensor
    local_rows = payload.shape[0]
    mean_load = local_rows * routes.shape[1] // experts
    slots = max(2, mean_load + (mean_load + 1) // 2)
    expert_ids = jnp.arange(experts, dtype=jnp.int32)
    chosen = jnp.any(routes[:, :, None] == expert_ids[None, None, :], axis=1)
    ranks = jnp.cumsum(chosen.astype(jnp.int32), axis=0) - 1
    slot_ids = jnp.arange(slots, dtype=jnp.int32)
    select = (chosen[:, :, None] & (ranks[:, :, None] == slot_ids[None, None, :])).astype(
        jnp.bfloat16
    )
    occupancy = jnp.sum(select.astype(jnp.float32), axis=0).astype(jnp.bfloat16)
    outgoing = jnp.einsum(
        "rec,rd->ecd", select, payload, preferred_element_type=jnp.float32
    ).astype(jnp.bfloat16)
    outgoing = outgoing.reshape(count_expert, count_tensor, slots, payload.shape[1])
    occupancy = occupancy.reshape(count_expert, count_tensor, slots)
    arrived, filled = (
        lax.all_to_all(
            lax.all_to_all(outgoing, "expert", split_axis=0, concat_axis=0, tiled=True),
            "tensor",
            split_axis=1,
            concat_axis=1,
            tiled=True,
        ),
        lax.all_to_all(
            lax.all_to_all(occupancy, "expert", split_axis=0, concat_axis=0, tiled=True),
            "tensor",
            split_axis=1,
            concat_axis=1,
            tiled=True,
        ),
    )
    rows = arrived.reshape(-1, payload.shape[1])
    count = jnp.sum(filled.astype(jnp.float32))
    return rows, count


def gather_rows(payload, routes):
    own = lax.axis_index("expert") * lax.axis_size("tensor") + lax.axis_index("tensor")
    named = lax.all_gather(routes, ("expert", "tensor"), axis=0, tiled=True)
    chosen = jnp.any(named == own, axis=1)
    rows = lax.all_gather(payload, ("expert", "tensor"), axis=0, tiled=True)
    count = jnp.sum(chosen.astype(jnp.float32))
    return rows, chosen, count


def on_device(attn_partial, residual, norm_gain, channel_order, rotation, routes, slab_block):
    summed = lax.psum_scatter(
        attn_partial[0].astype(jnp.float32).astype(jnp.bfloat16),
        "tensor",
        scatter_dimension=0,
        tiled=True,
    ).astype(jnp.float32)
    hidden = residual.astype(jnp.float32) + summed
    scale = lax.rsqrt(jnp.mean(hidden * hidden, axis=1, keepdims=True) + 1e-06)
    normed = (hidden * scale * norm_gain[None, :]).astype(jnp.bfloat16)
    payload = rotate_rows(normed, channel_order, rotation)
    experts = lax.axis_size("expert") * lax.axis_size("tensor")
    mean_load = residual.shape[0] * routes.shape[1] // experts
    slots = max(2, mean_load + (mean_load + 1) // 2)
    start = slab_block[0] * rotation.shape[1]
    if residual.shape[0] <= 4 * slots:
        rows, chosen, count = gather_rows(payload, routes)
        slab = lax.dynamic_slice_in_dim(rows, start, SLAB, 1)
        slab = slab * chosen[:, None].astype(slab.dtype)
    else:
        rows, count = dispatch_rows(payload, routes)
        slab = lax.dynamic_slice_in_dim(rows, start, SLAB, 1)
    product = lax.dot_general(
        rows, slab, (((0,), (0,)), ((), ())), preferred_element_type=jnp.float32
    )
    return (product * (2.0 / count)).astype(jnp.bfloat16)[None]


def solution(mesh):
    placed = (
        P("tensor", "expert", None),
        P(("expert", "tensor"), None),
        P(),
        P(),
        P(),
        P(("expert", "tensor"), None),
        P(("expert", "tensor")),
    )
    return jax.shard_map(
        on_device,
        mesh=mesh,
        in_specs=placed,
        out_specs=P(("expert", "tensor"), None, None),
        check_vma=False,
    )
```

```python
import functools

import jax
import jax.numpy as jnp
from jax import lax
from jax.experimental import pallas as pl
from jax.experimental.pallas import tpu as pltpu
from jax.sharding import PartitionSpec as P

SLAB = 512


def rotate_rows(rows, channel_order, rotation):
    moved = jnp.take(rows, channel_order, axis=1)
    blocks = moved.reshape(rows.shape[0], rotation.shape[0], rotation.shape[1])
    out = jnp.einsum("rbi,bij->rbj", blocks, rotation, preferred_element_type=jnp.float32)
    return out.reshape(rows.shape[0], -1).astype(jnp.bfloat16)


def dispatch_rows(payload, routes):
    count_expert = lax.axis_size("expert")
    count_tensor = lax.axis_size("tensor")
    experts = count_expert * count_tensor
    local_rows = payload.shape[0]
    mean_load = local_rows * routes.shape[1] // experts
    slots = max(2, mean_load + (mean_load + 1) // 2)
    expert_ids = jnp.arange(experts, dtype=jnp.int32)
    chosen = jnp.any(routes[:, :, None] == expert_ids[None, None, :], axis=1)
    ranks = jnp.cumsum(chosen.astype(jnp.int32), axis=0) - 1
    slot_ids = jnp.arange(slots, dtype=jnp.int32)
    select = (chosen[:, :, None] & (ranks[:, :, None] == slot_ids[None, None, :])).astype(
        jnp.bfloat16
    )
    occupancy = jnp.sum(select.astype(jnp.float32), axis=0).astype(jnp.bfloat16)
    outgoing = jnp.einsum(
        "rec,rd->ecd", select, payload, preferred_element_type=jnp.float32
    ).astype(jnp.bfloat16)
    outgoing = outgoing.reshape(count_expert, count_tensor, slots, payload.shape[1])
    occupancy = occupancy.reshape(count_expert, count_tensor, slots)
    arrived, filled = (
        lax.all_to_all(
            lax.all_to_all(outgoing, "expert", split_axis=0, concat_axis=0, tiled=True),
            "tensor",
            split_axis=1,
            concat_axis=1,
            tiled=True,
        ),
        lax.all_to_all(
            lax.all_to_all(occupancy, "expert", split_axis=0, concat_axis=0, tiled=True),
            "tensor",
            split_axis=1,
            concat_axis=1,
            tiled=True,
        ),
    )
    rows = arrived.reshape(-1, payload.shape[1])
    count = jnp.sum(filled.astype(jnp.float32))
    return rows, count


def line_order(length):
    orders = []
    for at in range(length):
        near = -1 if 2 * at < length else 1
        hops = [d for far in range(1, length) for d in (near * far, -near * far)]
        orders.append([at + d for d in hops if 0 <= at + d < length])
    return orders


def gram_kernel(
    planes, local, width, columns,
    bits_ref, own_ref, out_ref,
    rows, picked, moved, slab, total, staged, own_sem, send_sem, recv_sem, out_sem,
):
    expert, tensor = lax.axis_index("expert"), lax.axis_index("tensor")
    plane, side = lax.div(expert, 2), lax.rem(expert, 2)
    pair, core = lax.div(tensor, 2), lax.rem(tensor, 2)
    half = local // 2
    orders = line_order(planes)

    def table(values):
        total_of = 0
        for at, value in enumerate(values):
            total_of = total_of + value * lax.div(
                planes - lax.rem(plane + planes - at, planes), planes
            )
        return total_of

    def block(z, y, x, c):
        return (z * 2 + y) * 4 + x * 2 + c

    def device(z, y, x, c):
        return (z * 2 + y, x * 2 + c)

    def piece(number, h):
        return rows.at[pl.ds(pl.multiple_of(number * local + h * half, half), half), :]

    sends = []

    def send(number, h, target):
        copy = pltpu.make_async_remote_copy(
            src_ref=piece(number, h),
            dst_ref=piece(number, h),
            send_sem=send_sem.at[len(sends)],
            recv_sem=recv_sem.at[number, h],
            device_id=target,
            device_id_type=pl.DeviceIdType.MESH,
        )
        sends.append(copy)
        return copy

    def arrive(number, h):
        pltpu.make_async_remote_copy(
            src_ref=piece(number, h),
            dst_ref=piece(number, h),
            send_sem=send_sem.at[0],
            recv_sem=recv_sem.at[number, h],
            device_id=other_core,
            device_id_type=pl.DeviceIdType.MESH,
        ).wait_recv()

    other_pair = device(plane, side, 1 - pair, core)
    other_side = device(plane, 1 - side, pair, core)
    other_core = device(plane, side, pair, 1 - core)
    has_above = table([1 if at + 1 < planes else 0 for at in range(planes)])
    has_below = table([1 if at >= 1 else 0 for at in range(planes)])
    above = table([min(at + 1, planes - 1) for at in range(planes)])
    below = table([max(at - 1, 0) for at in range(planes)])

    fetch = pltpu.make_async_copy(
        own_ref,
        rows.at[pl.ds(pl.multiple_of(block(plane, side, pair, core) * local, local), local), :],
        own_sem,
    )
    fetch.start()

    barrier = pltpu.get_barrier_semaphore()
    for peer in (other_pair, other_side, other_core):
        pl.semaphore_signal(
            barrier, inc=1, device_id=peer, device_id_type=pl.DeviceIdType.MESH
        )

    @pl.when(has_above == 1)
    def _():
        pl.semaphore_signal(
            barrier, inc=1, device_id=device(above, side, pair, core),
            device_id_type=pl.DeviceIdType.MESH,
        )

    @pl.when(has_below == 1)
    def _():
        pl.semaphore_signal(
            barrier, inc=1, device_id=device(below, side, pair, core),
            device_id_type=pl.DeviceIdType.MESH,
        )

    pl.semaphore_wait(barrier, 3 + has_above + has_below)

    fetch.wait()

    conditional = []
    always = []

    def start(copy):
        always.append(copy)
        copy.start()

    def start_if(flag, copy):
        conditional.append((flag, copy))

        @pl.when(flag == 1)
        def _():
            copy.start()

    def spread(z):
        number = block(z, side, pair, core)
        start(send(number, 0, other_pair))
        start(send(number, 1, other_side))
        start(send(number, 1, other_pair))
        start(send(number, 0, other_side))
        for h in (0, 1):
            start(send(number, h, other_core))

    own = block(plane, side, pair, core)
    for h in (0, 1):
        start_if(has_above, send(own, h, device(above, side, pair, core)))
        start_if(has_below, send(own, h, device(below, side, pair, core)))
    spread(plane)

    def along(k):
        z = table([orders[at][k] for at in range(planes)])
        number = block(z, side, pair, core)
        has, target = [], []
        for at in range(planes):
            onward = at + 1 if orders[at][k] < at else at - 1
            has.append(1 if 0 <= onward < planes else 0)
            target.append(min(max(onward, 0), planes - 1))
        for h in (0, 1):
            arrive(number, h)
            start_if(table(has), send(number, h, device(table(target), side, pair, core)))
        spread(z)
        return z

    def first_halves(z):
        number = block(z, side, 1 - pair, core)
        arrive(number, 0)
        start(send(number, 0, other_side))
        start(send(number, 0, other_core))
        number = block(z, 1 - side, pair, core)
        arrive(number, 1)
        start(send(number, 1, other_pair))
        start(send(number, 1, other_core))

    me = expert * 4 + tensor
    tile = slab.shape[1]
    steps = width // tile
    span = tile // columns
    counted = jnp.zeros((1, 1), jnp.float32)

    def accumulate(z, y, first, last, counted):
        base = pl.multiple_of((z * 2 + y) * 4 * local, 4 * local)
        picked[...] = rows[pl.ds(base, 4 * local), :]
        named = picked[:, width:].astype(jnp.float32)
        lane = lax.broadcasted_iota(jnp.int32, named.shape, 1)
        chosen = jnp.sum(jnp.where(lane == me, named, 0.0), axis=1, keepdims=True)
        source = picked
        for bit in reversed(range(bits_ref.shape[0] // 2)):
            shift, stay, go = 1 << bit, bits_ref[2 * bit], bits_ref[2 * bit + 1]

            wanted = span + shift - 1
            both = wanted if source is moved else min(wanted, width // columns - shift)

            @pl.loop(0, both)
            def _(j):
                here = pl.ds(pl.multiple_of(j * columns, columns), columns)
                there = pl.ds(pl.multiple_of((j + shift) * columns, columns), columns)
                kept = source[:, here].reshape(-1, *stay.shape) * stay[None]
                taken = source[:, there].reshape(-1, *stay.shape) * go[None]
                moved[:, here] = (kept + taken).reshape(picked.shape[0], columns)

            if both < wanted:
                ends = slice(both * columns, wanted * columns)
                moved[:, ends] = source[:, ends]

            source = moved
        slab[...] = (source[:, :tile].astype(jnp.float32) * chosen).astype(jnp.bfloat16)
        counted = counted + jnp.sum(chosen, axis=0, keepdims=True)
        factor = 2.0 / counted

        @pl.loop(0, steps)
        def _(step):
            at = pl.ds(pl.multiple_of(step * tile, tile), tile)
            part = lax.dot_general(
                picked[:, at], slab[...], (((0,), (0,)), ((), ())),
                preferred_element_type=jnp.float32,
            )
            if first:
                total[at, :] = part
            elif not last:
                total[at, :] += part
            else:
                staged[at, :] = ((total[at, :] + part) * factor).astype(jnp.bfloat16)
                pltpu.make_async_copy(staged.at[at, :], out_ref.at[at, :], out_sem.at[step]).start()

        return counted

    seen = plane
    pending = None
    for k in range(planes):
        if k == 0:
            first_halves(seen)
        following = along(k) if k + 1 < planes else None
        if k > 0:
            first_halves(seen)
            counted = accumulate(pending, side, k == 1, False, counted)
            counted = accumulate(pending, 1 - side, False, False, counted)
        for number, h in (
            (block(seen, side, 1 - pair, core), 1),
            (block(seen, 1 - side, pair, core), 0),
        ):
            arrive(number, h)
            start(send(number, h, other_core))
        diagonal = block(seen, 1 - side, 1 - pair, core)
        for h in (0, 1):
            if k + 1 == planes and h == 0:
                for x in (0, 1):
                    number = block(seen, side, x, 1 - core)
                    arrive(number, 0)
                    arrive(number, 1)
                counted = accumulate(seen, side, planes == 1, False, counted)
            arrive(diagonal, h)
            start(send(diagonal, h, other_core))
        for y in (side, 1 - side):
            for x in (0, 1):
                if k + 1 < planes or y is not side:
                    number = block(seen, y, x, 1 - core)
                    arrive(number, 0)
                    arrive(number, 1)
        pending, seen = seen, following
    accumulate(pending, 1 - side, False, True, counted)

    for copy in always:
        copy.wait_send()
    for flag, copy in conditional:

        @pl.when(flag == 1)
        def _(copy=copy):
            copy.wait_send()

    @pl.loop(0, steps)
    def _(step):
        at = pl.ds(pl.multiple_of(step * tile, tile), tile)
        pltpu.make_async_copy(staged.at[at, :], out_ref.at[at, :], out_sem.at[step]).wait()


def gathered_gram(payload, routes, slab_block, columns):
    count_expert, count_tensor = lax.axis_size("expert"), lax.axis_size("tensor")
    experts, planes = count_expert * count_tensor, count_expert // 2
    local, width = payload.shape
    extra = -(-experts // 128) * 128
    expert_ids = jnp.arange(extra, dtype=jnp.int32)
    chosen = jnp.any(routes[:, :, None] == expert_ids[None, None, :], axis=1)
    own = jnp.concatenate([payload, chosen.astype(jnp.bfloat16)], axis=1)
    reach = width // columns - SLAB // columns
    levels = max(1, reach.bit_length())
    places = jnp.arange(levels)
    digits = (slab_block[0] >> places) & 1
    bits = jnp.stack([1 - digits, digits], axis=1).reshape(-1, 1, 1)
    bits = jnp.broadcast_to(bits, (2 * levels, 16, columns)).astype(jnp.bfloat16)
    most = SLAB // columns + 2 ** levels
    sends = planes * 14 + 2 * (planes + 1)
    return pl.pallas_call(
        functools.partial(gram_kernel, planes, local, width, columns),
        out_shape=jax.ShapeDtypeStruct((width, SLAB), jnp.bfloat16),
        in_specs=[
            pl.BlockSpec(memory_space=pltpu.VMEM),
            pl.BlockSpec(memory_space=pl.ANY),
        ],
        out_specs=pl.BlockSpec(memory_space=pl.ANY),
        scratch_shapes=[
            pltpu.VMEM((experts * local, width + extra), jnp.bfloat16),
            pltpu.VMEM((4 * local, width + extra), jnp.bfloat16),
            pltpu.VMEM((4 * local, most * columns // 2 + SLAB), jnp.bfloat16),
            pltpu.VMEM((4 * local, SLAB), jnp.bfloat16),
            pltpu.VMEM((width, SLAB), jnp.float32),
            pltpu.VMEM((width, SLAB), jnp.bfloat16),
            pltpu.SemaphoreType.DMA,
            pltpu.SemaphoreType.DMA((sends,)),
            pltpu.SemaphoreType.DMA((experts, 2)),
            pltpu.SemaphoreType.DMA((width // SLAB,)),
        ],
        compiler_params=pltpu.CompilerParams(
            collective_id=0, has_side_effects=True, vmem_limit_bytes=67043328
        ),
        name="gathered_gram",
    )(bits, own)


def on_device(attn_partial, residual, norm_gain, channel_order, rotation, routes, slab_block):
    summed = lax.psum_scatter(
        attn_partial[0].astype(jnp.float32).astype(jnp.bfloat16),
        "tensor",
        scatter_dimension=0,
        tiled=True,
    ).astype(jnp.float32)
    hidden = residual.astype(jnp.float32) + summed
    scale = lax.rsqrt(jnp.mean(hidden * hidden, axis=1, keepdims=True) + 1e-06)
    normed = (hidden * scale * norm_gain[None, :]).astype(jnp.bfloat16)
    payload = rotate_rows(normed, channel_order, rotation)
    experts = lax.axis_size("expert") * lax.axis_size("tensor")
    mean_load = residual.shape[0] * routes.shape[1] // experts
    slots = max(2, mean_load + (mean_load + 1) // 2)
    start = slab_block[0] * rotation.shape[1]
    if residual.shape[0] <= 4 * slots and lax.axis_size("tensor") == 4:
        return gathered_gram(payload, routes, slab_block, rotation.shape[1])[None]
    rows, count = dispatch_rows(payload, routes)
    slab = lax.dynamic_slice_in_dim(rows, start, SLAB, 1)
    product = lax.dot_general(
        rows, slab, (((0,), (0,)), ((), ())), preferred_element_type=jnp.float32
    )
    return (product * (2.0 / count)).astype(jnp.bfloat16)[None]


def solution(mesh):
    placed = (
        P("tensor", "expert", None),
        P(("expert", "tensor"), None),
        P(),
        P(),
        P(),
        P(("expert", "tensor"), None),
        P(("expert", "tensor")),
    )
    return jax.shard_map(
        on_device,
        mesh=mesh,
        in_specs=placed,
        out_specs=P(("expert", "tensor"), None, None),
        check_vma=False,
    )
```

```python
import functools

import jax
import jax.numpy as jnp
from jax import lax
from jax.experimental import pallas as pl
from jax.experimental.pallas import tpu as pltpu
from jax.sharding import PartitionSpec as P

SLAB = 512


def rotate_rows(rows, channel_order, rotation):
    moved = jnp.take(rows, channel_order, axis=1)
    blocks = moved.reshape(rows.shape[0], rotation.shape[0], rotation.shape[1])
    out = jnp.einsum("rbi,bij->rbj", blocks, rotation, preferred_element_type=jnp.float32)
    return out.reshape(rows.shape[0], -1).astype(jnp.bfloat16)


def dispatch_rows(payload, routes):
    count_expert = lax.axis_size("expert")
    count_tensor = lax.axis_size("tensor")
    experts = count_expert * count_tensor
    local_rows = payload.shape[0]
    mean_load = local_rows * routes.shape[1] // experts
    slots = max(2, mean_load + (mean_load + 1) // 2)
    expert_ids = jnp.arange(experts, dtype=jnp.int32)
    chosen = jnp.any(routes[:, :, None] == expert_ids[None, None, :], axis=1)
    ranks = jnp.cumsum(chosen.astype(jnp.int32), axis=0) - 1
    slot_ids = jnp.arange(slots, dtype=jnp.int32)
    select = (chosen[:, :, None] & (ranks[:, :, None] == slot_ids[None, None, :])).astype(
        jnp.bfloat16
    )
    occupancy = jnp.sum(select.astype(jnp.float32), axis=0).astype(jnp.bfloat16)
    outgoing = jnp.einsum(
        "rec,rd->ecd", select, payload, preferred_element_type=jnp.float32
    ).astype(jnp.bfloat16)
    outgoing = outgoing.reshape(count_expert, count_tensor, slots, payload.shape[1])
    occupancy = occupancy.reshape(count_expert, count_tensor, slots)
    arrived, filled = (
        lax.all_to_all(
            lax.all_to_all(outgoing, "expert", split_axis=0, concat_axis=0, tiled=True),
            "tensor",
            split_axis=1,
            concat_axis=1,
            tiled=True,
        ),
        lax.all_to_all(
            lax.all_to_all(occupancy, "expert", split_axis=0, concat_axis=0, tiled=True),
            "tensor",
            split_axis=1,
            concat_axis=1,
            tiled=True,
        ),
    )
    rows = arrived.reshape(-1, payload.shape[1])
    count = jnp.sum(filled.astype(jnp.float32))
    return rows, count


def line_order(length):
    orders = []
    for at in range(length):
        near = -1 if 2 * at < length else 1
        hops = [d for far in range(1, length) for d in (near * far, -near * far)]
        orders.append([at + d for d in hops if 0 <= at + d < length])
    return orders


def gram_kernel(
    planes, local, width, columns,
    bits_ref, own_ref, out_ref,
    rows, picked, moved, slab, total, staged, own_sem, send_sem, recv_sem, out_sem,
):
    expert, tensor = lax.axis_index("expert"), lax.axis_index("tensor")
    plane, side = lax.div(expert, 2), lax.rem(expert, 2)
    pair, core = lax.div(tensor, 2), lax.rem(tensor, 2)
    half = local // 2
    orders = line_order(planes)

    def table(values):
        total_of = 0
        for at, value in enumerate(values):
            total_of = total_of + value * lax.div(
                planes - lax.rem(plane + planes - at, planes), planes
            )
        return total_of

    def block(z, y, x, c):
        return (z * 2 + y) * 4 + x * 2 + c

    def device(z, y, x, c):
        return (z * 2 + y, x * 2 + c)

    def piece(number, h):
        return rows.at[pl.ds(pl.multiple_of(number * local + h * half, half), half), :]

    sends = []

    def send(number, h, target):
        copy = pltpu.make_async_remote_copy(
            src_ref=piece(number, h),
            dst_ref=piece(number, h),
            send_sem=send_sem.at[len(sends)],
            recv_sem=recv_sem.at[number, h],
            device_id=target,
            device_id_type=pl.DeviceIdType.MESH,
        )
        sends.append(copy)
        return copy

    def arrive(number, h):
        pltpu.make_async_remote_copy(
            src_ref=piece(number, h),
            dst_ref=piece(number, h),
            send_sem=send_sem.at[0],
            recv_sem=recv_sem.at[number, h],
            device_id=other_core,
            device_id_type=pl.DeviceIdType.MESH,
        ).wait_recv()

    other_pair = device(plane, side, 1 - pair, core)
    other_side = device(plane, 1 - side, pair, core)
    other_core = device(plane, side, pair, 1 - core)
    planes_by_turn = [
        table([orders[at][k] for at in range(planes)]) for k in range(planes - 1)
    ]

    fetch = pltpu.make_async_copy(
        own_ref,
        rows.at[pl.ds(pl.multiple_of(block(plane, side, pair, core) * local, local), local), :],
        own_sem,
    )
    fetch.start()

    barrier = pltpu.get_barrier_semaphore()
    peers = [other_pair, other_side, other_core]
    peers += [device(z, side, pair, core) for z in planes_by_turn]
    for peer in peers:
        pl.semaphore_signal(
            barrier, inc=1, device_id=peer, device_id_type=pl.DeviceIdType.MESH
        )
    pl.semaphore_wait(barrier, len(peers))

    fetch.wait()

    def spread(z):
        number = block(z, side, pair, core)
        send(number, 0, other_pair).start()
        send(number, 1, other_side).start()
        send(number, 1, other_pair).start()
        send(number, 0, other_side).start()
        for h in (0, 1):
            send(number, h, other_core).start()

    own = block(plane, side, pair, core)
    spread(plane)
    for z in planes_by_turn:
        for h in (0, 1):
            send(own, h, device(z, side, pair, core)).start()

    def along(k):
        z = planes_by_turn[k]
        for h in (0, 1):
            arrive(block(z, side, pair, core), h)
        spread(z)
        return z

    def first_halves(z):
        number = block(z, side, 1 - pair, core)
        arrive(number, 0)
        send(number, 0, other_side).start()
        send(number, 0, other_core).start()
        number = block(z, 1 - side, pair, core)
        arrive(number, 1)
        send(number, 1, other_pair).start()
        send(number, 1, other_core).start()

    me = expert * 4 + tensor
    tile = slab.shape[1]
    steps = width // tile
    span = tile // columns
    counted = jnp.zeros((1, 1), jnp.float32)

    def accumulate(z, y, first, last, counted):
        base = pl.multiple_of((z * 2 + y) * 4 * local, 4 * local)
        picked[...] = rows[pl.ds(base, 4 * local), :]
        named = picked[:, width:].astype(jnp.float32)
        lane = lax.broadcasted_iota(jnp.int32, named.shape, 1)
        chosen = jnp.sum(jnp.where(lane == me, named, 0.0), axis=1, keepdims=True)
        source = picked
        for bit in reversed(range(bits_ref.shape[0] // 2)):
            shift, stay, go = 1 << bit, bits_ref[2 * bit], bits_ref[2 * bit + 1]

            wanted = span + shift - 1
            both = wanted if source is moved else min(wanted, width // columns - shift)

            @pl.loop(0, both)
            def _(j):
                here = pl.ds(pl.multiple_of(j * columns, columns), columns)
                there = pl.ds(pl.multiple_of((j + shift) * columns, columns), columns)
                kept = source[:, here].reshape(-1, *stay.shape) * stay[None]
                taken = source[:, there].reshape(-1, *stay.shape) * go[None]
                moved[:, here] = (kept + taken).reshape(picked.shape[0], columns)

            if both < wanted:
                ends = slice(both * columns, wanted * columns)
                moved[:, ends] = source[:, ends]

            source = moved
        slab[...] = (source[:, :tile].astype(jnp.float32) * chosen).astype(jnp.bfloat16)
        counted = counted + jnp.sum(chosen, axis=0, keepdims=True)
        factor = 2.0 / counted

        @pl.loop(0, steps)
        def _(step):
            at = pl.ds(pl.multiple_of(step * tile, tile), tile)
            part = lax.dot_general(
                picked[:, at], slab[...], (((0,), (0,)), ((), ())),
                preferred_element_type=jnp.float32,
            )
            if first:
                total[at, :] = part
            elif not last:
                total[at, :] += part
            else:
                staged[at, :] = ((total[at, :] + part) * factor).astype(jnp.bfloat16)
                pltpu.make_async_copy(staged.at[at, :], out_ref.at[at, :], out_sem.at[step]).start()

        return counted

    def from_other_core(z, y):
        for x in (0, 1):
            for h in (0, 1):
                arrive(block(z, y, x, 1 - core), h)

    seen, before = plane, None
    for k in range(planes):
        first_halves(seen)
        if k > 0:
            counted = accumulate(before, 1 - side, False, False, counted)
        following = along(k) if k + 1 < planes else None
        for number, h in (
            (block(seen, side, 1 - pair, core), 1),
            (block(seen, 1 - side, pair, core), 0),
        ):
            arrive(number, h)
            send(number, h, other_core).start()
        from_other_core(seen, side)
        if k + 1 == planes:
            counted = accumulate(seen, side, k == 0, False, counted)
        for h in (0, 1):
            number = block(seen, 1 - side, 1 - pair, core)
            arrive(number, h)
            send(number, h, other_core).start()
        from_other_core(seen, 1 - side)
        if k + 1 < planes:
            counted = accumulate(seen, side, k == 0, False, counted)
        before, seen = seen, following
    accumulate(before, 1 - side, False, True, counted)

    for copy in sends:
        copy.wait_send()

    @pl.loop(0, steps)
    def _(step):
        at = pl.ds(pl.multiple_of(step * tile, tile), tile)
        pltpu.make_async_copy(staged.at[at, :], out_ref.at[at, :], out_sem.at[step]).wait()


def gathered_gram(payload, routes, slab_block, columns):
    count_expert, count_tensor = lax.axis_size("expert"), lax.axis_size("tensor")
    experts, planes = count_expert * count_tensor, count_expert // 2
    local, width = payload.shape
    extra = -(-experts // 128) * 128
    expert_ids = jnp.arange(extra, dtype=jnp.int32)
    chosen = jnp.any(routes[:, :, None] == expert_ids[None, None, :], axis=1)
    own = jnp.concatenate([payload, chosen.astype(jnp.bfloat16)], axis=1)
    reach = width // columns - SLAB // columns
    levels = max(1, reach.bit_length())
    places = jnp.arange(levels)
    digits = (slab_block[0] >> places) & 1
    bits = jnp.stack([1 - digits, digits], axis=1).reshape(-1, 1, 1)
    bits = jnp.broadcast_to(bits, (2 * levels, 16, columns)).astype(jnp.bfloat16)
    most = SLAB // columns + 2 ** levels
    sends = planes * 14 + 2 * (planes - 1)
    return pl.pallas_call(
        functools.partial(gram_kernel, planes, local, width, columns),
        out_shape=jax.ShapeDtypeStruct((width, SLAB), jnp.bfloat16),
        in_specs=[
            pl.BlockSpec(memory_space=pltpu.VMEM),
            pl.BlockSpec(memory_space=pl.ANY),
        ],
        out_specs=pl.BlockSpec(memory_space=pl.ANY),
        scratch_shapes=[
            pltpu.VMEM((experts * local, width + extra), jnp.bfloat16),
            pltpu.VMEM((4 * local, width + extra), jnp.bfloat16),
            pltpu.VMEM((4 * local, most * columns // 2 + SLAB), jnp.bfloat16),
            pltpu.VMEM((4 * local, SLAB), jnp.bfloat16),
            pltpu.VMEM((width, SLAB), jnp.float32),
            pltpu.VMEM((width, SLAB), jnp.bfloat16),
            pltpu.SemaphoreType.DMA,
            pltpu.SemaphoreType.DMA((sends,)),
            pltpu.SemaphoreType.DMA((experts, 2)),
            pltpu.SemaphoreType.DMA((width // SLAB,)),
        ],
        compiler_params=pltpu.CompilerParams(
            collective_id=0, has_side_effects=True, vmem_limit_bytes=67043328
        ),
        name="gathered_gram",
    )(bits, own)


def on_device(attn_partial, residual, norm_gain, channel_order, rotation, routes, slab_block):
    summed = lax.psum_scatter(
        attn_partial[0].astype(jnp.float32).astype(jnp.bfloat16),
        "tensor",
        scatter_dimension=0,
        tiled=True,
    ).astype(jnp.float32)
    hidden = residual.astype(jnp.float32) + summed
    scale = lax.rsqrt(jnp.mean(hidden * hidden, axis=1, keepdims=True) + 1e-06)
    normed = (hidden * scale * norm_gain[None, :]).astype(jnp.bfloat16)
    payload = rotate_rows(normed, channel_order, rotation)
    experts = lax.axis_size("expert") * lax.axis_size("tensor")
    mean_load = residual.shape[0] * routes.shape[1] // experts
    slots = max(2, mean_load + (mean_load + 1) // 2)
    start = slab_block[0] * rotation.shape[1]
    if residual.shape[0] <= 4 * slots and lax.axis_size("tensor") == 4:
        return gathered_gram(payload, routes, slab_block, rotation.shape[1])[None]
    rows, count = dispatch_rows(payload, routes)
    slab = lax.dynamic_slice_in_dim(rows, start, SLAB, 1)
    product = lax.dot_general(
        rows, slab, (((0,), (0,)), ((), ())), preferred_element_type=jnp.float32
    )
    return (product * (2.0 / count)).astype(jnp.bfloat16)[None]


def solution(mesh):
    placed = (
        P("tensor", "expert", None),
        P(("expert", "tensor"), None),
        P(),
        P(),
        P(),
        P(("expert", "tensor"), None),
        P(("expert", "tensor")),
    )
    return jax.shard_map(
        on_device,
        mesh=mesh,
        in_specs=placed,
        out_specs=P(("expert", "tensor"), None, None),
        check_vma=False,
    )
```

```python
import functools

import jax
import jax.numpy as jnp
from jax import lax
from jax.experimental import pallas as pl
from jax.experimental.pallas import tpu as pltpu
from jax.sharding import PartitionSpec as P

SLAB = 512


def rotate_rows(rows, channel_order, rotation):
    moved = jnp.take(rows, channel_order, axis=1)
    blocks = moved.reshape(rows.shape[0], rotation.shape[0], rotation.shape[1])
    out = jnp.einsum("rbi,bij->rbj", blocks, rotation, preferred_element_type=jnp.float32)
    return out.reshape(rows.shape[0], -1).astype(jnp.bfloat16)


def dispatch_rows(payload, routes):
    count_expert = lax.axis_size("expert")
    count_tensor = lax.axis_size("tensor")
    experts = count_expert * count_tensor
    local_rows = payload.shape[0]
    mean_load = local_rows * routes.shape[1] // experts
    slots = max(2, mean_load + (mean_load + 1) // 2)
    expert_ids = jnp.arange(experts, dtype=jnp.int32)
    chosen = jnp.any(routes[:, :, None] == expert_ids[None, None, :], axis=1)
    ranks = jnp.cumsum(chosen.astype(jnp.int32), axis=0) - 1
    slot_ids = jnp.arange(slots, dtype=jnp.int32)
    select = (chosen[:, :, None] & (ranks[:, :, None] == slot_ids[None, None, :])).astype(
        jnp.bfloat16
    )
    occupancy = jnp.sum(select.astype(jnp.float32), axis=0).astype(jnp.bfloat16)
    outgoing = jnp.einsum(
        "rec,rd->ecd", select, payload, preferred_element_type=jnp.float32
    ).astype(jnp.bfloat16)
    outgoing = outgoing.reshape(count_expert, count_tensor, slots, payload.shape[1])
    occupancy = occupancy.reshape(count_expert, count_tensor, slots)
    arrived, filled = (
        lax.all_to_all(
            lax.all_to_all(outgoing, "expert", split_axis=0, concat_axis=0, tiled=True),
            "tensor",
            split_axis=1,
            concat_axis=1,
            tiled=True,
        ),
        lax.all_to_all(
            lax.all_to_all(occupancy, "expert", split_axis=0, concat_axis=0, tiled=True),
            "tensor",
            split_axis=1,
            concat_axis=1,
            tiled=True,
        ),
    )
    rows = arrived.reshape(-1, payload.shape[1])
    count = jnp.sum(filled.astype(jnp.float32))
    return rows, count


def line_order(length):
    orders = []
    for at in range(length):
        near = -1 if 2 * at < length else 1
        hops = [d for far in range(1, length) for d in (near * far, -near * far)]
        orders.append([at + d for d in hops if 0 <= at + d < length])
    return orders


def gram_kernel(
    planes, local, width, columns,
    bits_ref, own_ref, out_ref,
    rows, picked, moved, slab, total, staged, own_sem, send_sem, recv_sem, out_sem,
):
    expert, tensor = lax.axis_index("expert"), lax.axis_index("tensor")
    plane, side = lax.div(expert, 2), lax.rem(expert, 2)
    pair, core = lax.div(tensor, 2), lax.rem(tensor, 2)
    half = local // 2
    orders = line_order(planes)

    def table(values):
        total_of = 0
        for at, value in enumerate(values):
            total_of = total_of + value * lax.div(
                planes - lax.rem(plane + planes - at, planes), planes
            )
        return total_of

    def block(z, y, x, c):
        return (z * 2 + y) * 4 + x * 2 + c

    def device(z, y, x, c):
        return (z * 2 + y, x * 2 + c)

    def piece(number, h):
        return rows.at[pl.ds(pl.multiple_of(number * local + h * half, half), half), :]

    sends = []

    def send(number, h, target):
        copy = pltpu.make_async_remote_copy(
            src_ref=piece(number, h),
            dst_ref=piece(number, h),
            send_sem=send_sem.at[len(sends) + len(conditional)],
            recv_sem=recv_sem.at[number, h],
            device_id=target,
            device_id_type=pl.DeviceIdType.MESH,
        )
        sends.append(copy)
        return copy

    def arrive(number, h):
        pltpu.make_async_remote_copy(
            src_ref=piece(number, h),
            dst_ref=piece(number, h),
            send_sem=send_sem.at[0],
            recv_sem=recv_sem.at[number, h],
            device_id=other_core,
            device_id_type=pl.DeviceIdType.MESH,
        ).wait_recv()

    other_pair = device(plane, side, 1 - pair, core)
    other_side = device(plane, 1 - side, pair, core)
    other_core = device(plane, side, pair, 1 - core)
    planes_by_turn = [
        table([orders[at][k] for at in range(planes)]) for k in range(planes - 1)
    ]

    def beside(step):
        there = table([1 if 0 <= at + step < planes else 0 for at in range(planes)])
        return there, table([min(max(at + step, 0), planes - 1) for at in range(planes)])

    conditional = []

    def send_if(flag, number, h, z):
        copy = send(number, h, device(z, side, pair, core))
        sends.pop()
        conditional.append((flag, copy))

        @pl.when(flag == 1)
        def _():
            copy.start()

    fetch = pltpu.make_async_copy(
        own_ref,
        rows.at[pl.ds(pl.multiple_of(block(plane, side, pair, core) * local, local), local), :],
        own_sem,
    )
    fetch.start()

    barrier = pltpu.get_barrier_semaphore()
    barrier_wait = 3
    for peer in (other_pair, other_side, other_core):
        pl.semaphore_signal(
            barrier, inc=1, device_id=peer, device_id_type=pl.DeviceIdType.MESH
        )
    for step in (-1, 1):
        there, z = beside(step)
        barrier_wait = barrier_wait + there

        @pl.when(there == 1)
        def _():
            pl.semaphore_signal(
                barrier, inc=1, device_id=device(z, side, pair, core),
                device_id_type=pl.DeviceIdType.MESH,
            )

    pl.semaphore_wait(barrier, barrier_wait)

    fetch.wait()

    def spread(z):
        number = block(z, side, pair, core)
        send(number, 0, other_pair).start()
        send(number, 1, other_side).start()
        send(number, 1, other_pair).start()
        send(number, 0, other_side).start()
        for h in (0, 1):
            send(number, h, other_core).start()

    own = block(plane, side, pair, core)
    spread(plane)
    for h in (0, 1):
        for step in (-1, 1):
            there, z = beside(step)
            send_if(there, own, h, z)

    def take(far):
        for h in (0, 1):
            for step in (-1, 1):
                there, z = beside(step * far)
                onward, target = beside(-step)
                number = block(z, side, pair, core)

                @pl.when(there == 1)
                def _():
                    arrive(number, h)

                send_if(there * onward, number, h, target)

    def along(k):
        take(k + 1)
        z = planes_by_turn[k]
        spread(z)
        return z

    def first_halves(z):
        number = block(z, side, 1 - pair, core)
        arrive(number, 0)
        send(number, 0, other_side).start()
        send(number, 0, other_core).start()
        number = block(z, 1 - side, pair, core)
        arrive(number, 1)
        send(number, 1, other_pair).start()
        send(number, 1, other_core).start()

    me = expert * 4 + tensor
    tile = slab.shape[1]
    steps = width // tile
    span = tile // columns
    counted = jnp.zeros((1, 1), jnp.float32)

    def accumulate(z, y, first, last, counted):
        base = pl.multiple_of((z * 2 + y) * 4 * local, 4 * local)
        picked[...] = rows[pl.ds(base, 4 * local), :]
        named = picked[:, width:].astype(jnp.float32)
        lane = lax.broadcasted_iota(jnp.int32, named.shape, 1)
        chosen = jnp.sum(jnp.where(lane == me, named, 0.0), axis=1, keepdims=True)
        source = picked
        for bit in reversed(range(bits_ref.shape[0] // 2)):
            shift, stay, go = 1 << bit, bits_ref[2 * bit], bits_ref[2 * bit + 1]

            wanted = span + shift - 1
            both = wanted if source is moved else min(wanted, width // columns - shift)

            @pl.loop(0, both)
            def _(j):
                here = pl.ds(pl.multiple_of(j * columns, columns), columns)
                there = pl.ds(pl.multiple_of((j + shift) * columns, columns), columns)
                kept = source[:, here].reshape(-1, *stay.shape) * stay[None]
                taken = source[:, there].reshape(-1, *stay.shape) * go[None]
                moved[:, here] = (kept + taken).reshape(picked.shape[0], columns)

            if both < wanted:
                ends = slice(both * columns, wanted * columns)
                moved[:, ends] = source[:, ends]

            source = moved
        slab[...] = (source[:, :tile].astype(jnp.float32) * chosen).astype(jnp.bfloat16)
        counted = counted + jnp.sum(chosen, axis=0, keepdims=True)
        factor = 2.0 / counted

        @pl.loop(0, steps)
        def _(step):
            at = pl.ds(pl.multiple_of(step * tile, tile), tile)
            part = lax.dot_general(
                picked[:, at], slab[...], (((0,), (0,)), ((), ())),
                preferred_element_type=jnp.float32,
            )
            if first:
                total[at, :] = part
            elif not last:
                total[at, :] += part
            else:
                staged[at, :] = ((total[at, :] + part) * factor).astype(jnp.bfloat16)
                pltpu.make_async_copy(staged.at[at, :], out_ref.at[at, :], out_sem.at[step]).start()

        return counted

    def from_other_core(z, y):
        for x in (0, 1):
            for h in (0, 1):
                arrive(block(z, y, x, 1 - core), h)

    seen, before = plane, None
    for k in range(planes):
        first_halves(seen)
        if k > 0:
            counted = accumulate(before, 1 - side, False, False, counted)
        following = along(k) if k + 1 < planes else None
        for number, h in (
            (block(seen, side, 1 - pair, core), 1),
            (block(seen, 1 - side, pair, core), 0),
        ):
            arrive(number, h)
            send(number, h, other_core).start()
        from_other_core(seen, side)
        if k + 1 == planes:
            counted = accumulate(seen, side, k == 0, False, counted)
        for h in (0, 1):
            number = block(seen, 1 - side, 1 - pair, core)
            arrive(number, h)
            send(number, h, other_core).start()
        from_other_core(seen, 1 - side)
        if k + 1 < planes:
            counted = accumulate(seen, side, k == 0, False, counted)
        before, seen = seen, following
    accumulate(before, 1 - side, False, True, counted)

    for copy in sends:
        copy.wait_send()
    for flag, copy in conditional:

        @pl.when(flag == 1)
        def _(copy=copy):
            copy.wait_send()

    @pl.loop(0, steps)
    def _(step):
        at = pl.ds(pl.multiple_of(step * tile, tile), tile)
        pltpu.make_async_copy(staged.at[at, :], out_ref.at[at, :], out_sem.at[step]).wait()


def gathered_gram(payload, routes, slab_block, columns):
    count_expert, count_tensor = lax.axis_size("expert"), lax.axis_size("tensor")
    experts, planes = count_expert * count_tensor, count_expert // 2
    local, width = payload.shape
    extra = -(-experts // 128) * 128
    expert_ids = jnp.arange(extra, dtype=jnp.int32)
    chosen = jnp.any(routes[:, :, None] == expert_ids[None, None, :], axis=1)
    own = jnp.concatenate([payload, chosen.astype(jnp.bfloat16)], axis=1)
    reach = width // columns - SLAB // columns
    levels = max(1, reach.bit_length())
    places = jnp.arange(levels)
    digits = (slab_block[0] >> places) & 1
    bits = jnp.stack([1 - digits, digits], axis=1).reshape(-1, 1, 1)
    bits = jnp.broadcast_to(bits, (2 * levels, 16, columns)).astype(jnp.bfloat16)
    most = SLAB // columns + 2 ** levels
    sends = planes * 14 + planes * 4
    return pl.pallas_call(
        functools.partial(gram_kernel, planes, local, width, columns),
        out_shape=jax.ShapeDtypeStruct((width, SLAB), jnp.bfloat16),
        in_specs=[
            pl.BlockSpec(memory_space=pltpu.VMEM),
            pl.BlockSpec(memory_space=pl.ANY),
        ],
        out_specs=pl.BlockSpec(memory_space=pl.ANY),
        scratch_shapes=[
            pltpu.VMEM((experts * local, width + extra), jnp.bfloat16),
            pltpu.VMEM((4 * local, width + extra), jnp.bfloat16),
            pltpu.VMEM((4 * local, most * columns // 2 + SLAB), jnp.bfloat16),
            pltpu.VMEM((4 * local, SLAB), jnp.bfloat16),
            pltpu.VMEM((width, SLAB), jnp.float32),
            pltpu.VMEM((width, SLAB), jnp.bfloat16),
            pltpu.SemaphoreType.DMA,
            pltpu.SemaphoreType.DMA((sends,)),
            pltpu.SemaphoreType.DMA((experts, 2)),
            pltpu.SemaphoreType.DMA((width // SLAB,)),
        ],
        compiler_params=pltpu.CompilerParams(
            collective_id=0, has_side_effects=True, vmem_limit_bytes=67043328
        ),
        name="gathered_gram",
    )(bits, own)


def normed_kernel(
    local, partial_ref, residual_ref, gain_ref, out_ref,
    mine, got, mid, far, own_sem, core_send, core_recv, pair_send, pair_recv,
):
    expert, tensor = lax.axis_index("expert"), lax.axis_index("tensor")
    pair, core = lax.div(tensor, 2), lax.rem(tensor, 2)
    other_core = (expert, pair * 2 + 1 - core)
    other_pair = (expert, (1 - pair) * 2 + core)
    parts = 4
    size = local // parts

    def source(p, c, at, count):
        start = pl.multiple_of((p * 2 + c) * local + at, size)
        return partial_ref.at[0, pl.ds(start, count), :]

    loads = []
    for turn, p in enumerate((1 - pair, pair)):
        loads.append(pltpu.make_async_copy(source(p, core, 0, local), mine.at[turn], own_sem.at[turn]))
        loads[-1].start()

    barrier = pltpu.get_barrier_semaphore()
    for peer in (other_core, other_pair):
        pl.semaphore_signal(
            barrier, inc=1, device_id=peer, device_id_type=pl.DeviceIdType.MESH
        )
    pl.semaphore_wait(barrier, 2)

    inside = []
    for turn, p in enumerate((1 - pair, pair)):
        for part in range(parts):
            rows = pl.ds(part * size, size)
            number = turn * parts + part
            inside.append(
                pltpu.make_async_remote_copy(
                    src_ref=source(p, 1 - core, part * size, size),
                    dst_ref=got.at[turn, rows, :],
                    send_sem=core_send.at[number],
                    recv_sem=core_recv.at[number],
                    device_id=other_core,
                    device_id_type=pl.DeviceIdType.MESH,
                )
            )
            inside[-1].start()

    across = []
    loads[0].wait()
    for part in range(parts):
        rows = pl.ds(part * size, size)
        inside[part].wait_recv()
        mid[rows, :] = (
            mine[0, rows, :].astype(jnp.float32) + got[0, rows, :].astype(jnp.float32)
        ).astype(jnp.bfloat16)
        across.append(
            pltpu.make_async_remote_copy(
                src_ref=mid.at[rows, :],
                dst_ref=far.at[rows, :],
                send_sem=pair_send.at[part],
                recv_sem=pair_recv.at[part],
                device_id=other_pair,
                device_id_type=pl.DeviceIdType.MESH,
            )
        )
        if part > 0:
            across[part - 1].start()
    loads[1].wait()
    for part in range(parts):
        inside[parts + part].wait_recv()
    across[parts - 1].start()

    for part in range(parts):
        rows = pl.ds(part * size, size)
        across[part].wait_recv()
        attn = (
            mine[1, rows, :].astype(jnp.float32)
            + got[1, rows, :].astype(jnp.float32)
            + far[rows, :].astype(jnp.float32)
        )
        hidden = residual_ref[rows, :].astype(jnp.float32) + attn
        scale = lax.rsqrt(jnp.mean(hidden * hidden, axis=1, keepdims=True) + 1e-06)
        out_ref[rows, :] = (hidden * scale * gain_ref[...]).astype(jnp.bfloat16)

    for copy in inside + across:
        copy.wait_send()


def normed_rows(attn_partial, residual, norm_gain):
    local, width = residual.shape
    return pl.pallas_call(
        functools.partial(normed_kernel, local),
        out_shape=jax.ShapeDtypeStruct((local, width), jnp.bfloat16),
        in_specs=[
            pl.BlockSpec(memory_space=pl.ANY),
            pl.BlockSpec(memory_space=pltpu.VMEM),
            pl.BlockSpec(memory_space=pltpu.VMEM),
        ],
        out_specs=pl.BlockSpec(memory_space=pltpu.VMEM),
        scratch_shapes=[
            pltpu.VMEM((2, local, width), jnp.bfloat16),
            pltpu.VMEM((2, local, width), jnp.bfloat16),
            pltpu.VMEM((local, width), jnp.bfloat16),
            pltpu.VMEM((local, width), jnp.bfloat16),
            pltpu.SemaphoreType.DMA((2,)),
            pltpu.SemaphoreType.DMA((8,)),
            pltpu.SemaphoreType.DMA((8,)),
            pltpu.SemaphoreType.DMA((4,)),
            pltpu.SemaphoreType.DMA((4,)),
        ],
        compiler_params=pltpu.CompilerParams(collective_id=1, has_side_effects=True),
        name="normed_rows",
    )(attn_partial, residual, norm_gain[None, :])


def on_device(attn_partial, residual, norm_gain, channel_order, rotation, routes, slab_block):
    experts = lax.axis_size("expert") * lax.axis_size("tensor")
    mean_load = residual.shape[0] * routes.shape[1] // experts
    slots = max(2, mean_load + (mean_load + 1) // 2)
    spread_all = residual.shape[0] <= 4 * slots and lax.axis_size("tensor") == 4
    if spread_all:
        normed = normed_rows(attn_partial, residual, norm_gain)
    else:
        summed = lax.psum_scatter(
            attn_partial[0].astype(jnp.float32).astype(jnp.bfloat16),
            "tensor",
            scatter_dimension=0,
            tiled=True,
        ).astype(jnp.float32)
        hidden = residual.astype(jnp.float32) + summed
        scale = lax.rsqrt(jnp.mean(hidden * hidden, axis=1, keepdims=True) + 1e-06)
        normed = (hidden * scale * norm_gain[None, :]).astype(jnp.bfloat16)
    payload = rotate_rows(normed, channel_order, rotation)
    start = slab_block[0] * rotation.shape[1]
    if spread_all:
        return gathered_gram(payload, routes, slab_block, rotation.shape[1])[None]
    rows, count = dispatch_rows(payload, routes)
    slab = lax.dynamic_slice_in_dim(rows, start, SLAB, 1)
    product = lax.dot_general(
        rows, slab, (((0,), (0,)), ((), ())), preferred_element_type=jnp.float32
    )
    return (product * (2.0 / count)).astype(jnp.bfloat16)[None]


def solution(mesh):
    placed = (
        P("tensor", "expert", None),
        P(("expert", "tensor"), None),
        P(),
        P(),
        P(),
        P(("expert", "tensor"), None),
        P(("expert", "tensor")),
    )
    return jax.shard_map(
        on_device,
        mesh=mesh,
        in_specs=placed,
        out_specs=P(("expert", "tensor"), None, None),
        check_vma=False,
    )
```

```python
import functools

import jax
import jax.numpy as jnp
from jax import lax
from jax.experimental import pallas as pl
from jax.experimental.pallas import tpu as pltpu
from jax.sharding import PartitionSpec as P

SLAB = 512


def rotate_rows(rows, channel_order, rotation):
    moved = jnp.take(rows, channel_order, axis=1)
    blocks = moved.reshape(rows.shape[0], rotation.shape[0], rotation.shape[1])
    out = jnp.einsum("rbi,bij->rbj", blocks, rotation, preferred_element_type=jnp.float32)
    return out.reshape(rows.shape[0], -1).astype(jnp.bfloat16)


def dispatch_rows(payload, routes):
    count_expert = lax.axis_size("expert")
    count_tensor = lax.axis_size("tensor")
    experts = count_expert * count_tensor
    local_rows = payload.shape[0]
    mean_load = local_rows * routes.shape[1] // experts
    slots = max(2, mean_load + (mean_load + 1) // 2)
    expert_ids = jnp.arange(experts, dtype=jnp.int32)
    chosen = jnp.any(routes[:, :, None] == expert_ids[None, None, :], axis=1)
    ranks = jnp.cumsum(chosen.astype(jnp.int32), axis=0) - 1
    slot_ids = jnp.arange(slots, dtype=jnp.int32)
    select = (chosen[:, :, None] & (ranks[:, :, None] == slot_ids[None, None, :])).astype(
        jnp.bfloat16
    )
    occupancy = jnp.sum(select.astype(jnp.float32), axis=0).astype(jnp.bfloat16)
    outgoing = jnp.einsum(
        "rec,rd->ecd", select, payload, preferred_element_type=jnp.float32
    ).astype(jnp.bfloat16)
    outgoing = outgoing.reshape(count_expert, count_tensor, slots, payload.shape[1])
    occupancy = occupancy.reshape(count_expert, count_tensor, slots)
    arrived, filled = (
        lax.all_to_all(
            lax.all_to_all(outgoing, "expert", split_axis=0, concat_axis=0, tiled=True),
            "tensor",
            split_axis=1,
            concat_axis=1,
            tiled=True,
        ),
        lax.all_to_all(
            lax.all_to_all(occupancy, "expert", split_axis=0, concat_axis=0, tiled=True),
            "tensor",
            split_axis=1,
            concat_axis=1,
            tiled=True,
        ),
    )
    rows = arrived.reshape(-1, payload.shape[1])
    count = jnp.sum(filled.astype(jnp.float32))
    return rows, count


def line_order(length):
    orders = []
    for at in range(length):
        near = -1 if 2 * at < length else 1
        hops = [d for far in range(1, length) for d in (near * far, -near * far)]
        orders.append([at + d for d in hops if 0 <= at + d < length])
    return orders


def gram_kernel(
    planes, local, width, columns,
    bits_ref, own_ref, out_ref,
    rows, picked, moved, slab, total, staged, own_sem, send_sem, recv_sem, out_sem,
):
    expert, tensor = lax.axis_index("expert"), lax.axis_index("tensor")
    plane, side = lax.div(expert, 2), lax.rem(expert, 2)
    pair, core = lax.div(tensor, 2), lax.rem(tensor, 2)
    half = local // 2
    orders = line_order(planes)

    def table(values):
        total_of = 0
        for at, value in enumerate(values):
            total_of = total_of + value * lax.div(
                planes - lax.rem(plane + planes - at, planes), planes
            )
        return total_of

    def block(z, y, x, c):
        return (z * 2 + y) * 4 + x * 2 + c

    def device(z, y, x, c):
        return (z * 2 + y, x * 2 + c)

    def piece(number, h):
        return rows.at[pl.ds(pl.multiple_of(number * local + h * half, half), half), :]

    sends = []

    def send(number, h, target):
        copy = pltpu.make_async_remote_copy(
            src_ref=piece(number, h),
            dst_ref=piece(number, h),
            send_sem=send_sem.at[len(sends) + len(conditional)],
            recv_sem=recv_sem.at[number, h],
            device_id=target,
            device_id_type=pl.DeviceIdType.MESH,
        )
        sends.append(copy)
        return copy

    def arrive(number, h):
        pltpu.make_async_remote_copy(
            src_ref=piece(number, h),
            dst_ref=piece(number, h),
            send_sem=send_sem.at[0],
            recv_sem=recv_sem.at[number, h],
            device_id=other_core,
            device_id_type=pl.DeviceIdType.MESH,
        ).wait_recv()

    other_pair = device(plane, side, 1 - pair, core)
    other_side = device(plane, 1 - side, pair, core)
    other_core = device(plane, side, pair, 1 - core)
    planes_by_turn = [
        table([orders[at][k] for at in range(planes)]) for k in range(planes - 1)
    ]

    def beside(step):
        there = table([1 if 0 <= at + step < planes else 0 for at in range(planes)])
        return there, table([min(max(at + step, 0), planes - 1) for at in range(planes)])

    conditional = []

    def send_if(flag, number, h, z):
        copy = send(number, h, device(z, side, pair, core))
        sends.pop()
        conditional.append((flag, copy))

        @pl.when(flag == 1)
        def _():
            copy.start()

    fetch = pltpu.make_async_copy(
        own_ref,
        rows.at[pl.ds(pl.multiple_of(block(plane, side, pair, core) * local, local), local), :],
        own_sem,
    )
    fetch.start()

    barrier = pltpu.get_barrier_semaphore()
    barrier_wait = 3
    for peer in (other_pair, other_side, other_core):
        pl.semaphore_signal(
            barrier, inc=1, device_id=peer, device_id_type=pl.DeviceIdType.MESH
        )
    for step in (-1, 1):
        there, z = beside(step)
        barrier_wait = barrier_wait + there

        @pl.when(there == 1)
        def _():
            pl.semaphore_signal(
                barrier, inc=1, device_id=device(z, side, pair, core),
                device_id_type=pl.DeviceIdType.MESH,
            )

    pl.semaphore_wait(barrier, barrier_wait)

    fetch.wait()

    def spread(z):
        number = block(z, side, pair, core)
        send(number, 0, other_pair).start()
        send(number, 1, other_side).start()
        send(number, 1, other_pair).start()
        send(number, 0, other_side).start()
        for h in (0, 1):
            send(number, h, other_core).start()

    own = block(plane, side, pair, core)
    spread(plane)
    for h in (0, 1):
        for step in (-1, 1):
            there, z = beside(step)
            send_if(there, own, h, z)

    def take(far):
        for h in (0, 1):
            for step in (-1, 1):
                there, z = beside(step * far)
                onward, target = beside(-step)
                number = block(z, side, pair, core)

                @pl.when(there == 1)
                def _():
                    arrive(number, h)

                send_if(there * onward, number, h, target)

    def along(k):
        take(k + 1)
        z = planes_by_turn[k]
        spread(z)
        return z

    def first_halves(z):
        number = block(z, side, 1 - pair, core)
        arrive(number, 0)
        send(number, 0, other_side).start()
        send(number, 0, other_core).start()
        number = block(z, 1 - side, pair, core)
        arrive(number, 1)
        send(number, 1, other_pair).start()
        send(number, 1, other_core).start()

    me = expert * 4 + tensor
    tile = slab.shape[1]
    steps = width // tile
    span = tile // columns
    counted = jnp.zeros((1, 1), jnp.float32)

    def accumulate(z, y, first, last, counted):
        base = pl.multiple_of((z * 2 + y) * 4 * local, 4 * local)
        picked[...] = rows[pl.ds(base, 4 * local), :]
        named = picked[:, width:].astype(jnp.float32)
        lane = lax.broadcasted_iota(jnp.int32, named.shape, 1)
        chosen = jnp.sum(jnp.where(lane == me, named, 0.0), axis=1, keepdims=True)
        source = picked
        for bit in reversed(range(bits_ref.shape[0] // 2)):
            shift, stay, go = 1 << bit, bits_ref[2 * bit], bits_ref[2 * bit + 1]

            wanted = span + shift - 1
            both = wanted if source is moved else min(wanted, width // columns - shift)

            @pl.loop(0, both)
            def _(j):
                here = pl.ds(pl.multiple_of(j * columns, columns), columns)
                there = pl.ds(pl.multiple_of((j + shift) * columns, columns), columns)
                kept = source[:, here].reshape(-1, *stay.shape) * stay[None]
                taken = source[:, there].reshape(-1, *stay.shape) * go[None]
                moved[:, here] = (kept + taken).reshape(picked.shape[0], columns)

            if both < wanted:
                ends = slice(both * columns, wanted * columns)
                moved[:, ends] = source[:, ends]

            source = moved
        slab[...] = (source[:, :tile].astype(jnp.float32) * chosen).astype(jnp.bfloat16)
        counted = counted + jnp.sum(chosen, axis=0, keepdims=True)
        factor = 2.0 / counted

        @pl.loop(0, steps)
        def _(step):
            at = pl.ds(pl.multiple_of(step * tile, tile), tile)
            part = lax.dot_general(
                picked[:, at], slab[...], (((0,), (0,)), ((), ())),
                preferred_element_type=jnp.float32,
            )
            if first:
                total[at, :] = part
            elif not last:
                total[at, :] += part
            else:
                staged[at, :] = ((total[at, :] + part) * factor).astype(jnp.bfloat16)
                pltpu.make_async_copy(staged.at[at, :], out_ref.at[at, :], out_sem.at[step]).start()

        return counted

    def from_other_core(z, y):
        for x in (0, 1):
            for h in (0, 1):
                arrive(block(z, y, x, 1 - core), h)

    seen, before = plane, None
    for k in range(planes):
        first_halves(seen)
        if k > 0:
            counted = accumulate(before, 1 - side, False, False, counted)
        following = along(k) if k + 1 < planes else None
        for number, h in (
            (block(seen, side, 1 - pair, core), 1),
            (block(seen, 1 - side, pair, core), 0),
        ):
            arrive(number, h)
            send(number, h, other_core).start()
        from_other_core(seen, side)
        if k + 1 == planes:
            counted = accumulate(seen, side, k == 0, False, counted)
        for h in (0, 1):
            number = block(seen, 1 - side, 1 - pair, core)
            arrive(number, h)
            send(number, h, other_core).start()
        from_other_core(seen, 1 - side)
        if k + 1 < planes:
            counted = accumulate(seen, side, k == 0, False, counted)
        before, seen = seen, following
    accumulate(before, 1 - side, False, True, counted)

    for copy in sends:
        copy.wait_send()
    for flag, copy in conditional:

        @pl.when(flag == 1)
        def _(copy=copy):
            copy.wait_send()

    @pl.loop(0, steps)
    def _(step):
        at = pl.ds(pl.multiple_of(step * tile, tile), tile)
        pltpu.make_async_copy(staged.at[at, :], out_ref.at[at, :], out_sem.at[step]).wait()


def gathered_gram(payload, routes, slab_block, columns):
    count_expert, count_tensor = lax.axis_size("expert"), lax.axis_size("tensor")
    experts, planes = count_expert * count_tensor, count_expert // 2
    local, width = payload.shape
    extra = -(-experts // 128) * 128
    expert_ids = jnp.arange(extra, dtype=jnp.int32)
    chosen = jnp.any(routes[:, :, None] == expert_ids[None, None, :], axis=1)
    own = jnp.concatenate([payload, chosen.astype(jnp.bfloat16)], axis=1)
    reach = width // columns - SLAB // columns
    levels = max(1, reach.bit_length())
    places = jnp.arange(levels)
    digits = (slab_block[0] >> places) & 1
    bits = jnp.stack([1 - digits, digits], axis=1).reshape(-1, 1, 1)
    bits = jnp.broadcast_to(bits, (2 * levels, 16, columns)).astype(jnp.bfloat16)
    most = SLAB // columns + 2 ** levels
    sends = planes * 14 + planes * 4
    return pl.pallas_call(
        functools.partial(gram_kernel, planes, local, width, columns),
        out_shape=jax.ShapeDtypeStruct((width, SLAB), jnp.bfloat16),
        in_specs=[
            pl.BlockSpec(memory_space=pltpu.VMEM),
            pl.BlockSpec(memory_space=pl.ANY),
        ],
        out_specs=pl.BlockSpec(memory_space=pl.ANY),
        scratch_shapes=[
            pltpu.VMEM((experts * local, width + extra), jnp.bfloat16),
            pltpu.VMEM((4 * local, width + extra), jnp.bfloat16),
            pltpu.VMEM((4 * local, most * columns // 2 + SLAB), jnp.bfloat16),
            pltpu.VMEM((4 * local, SLAB), jnp.bfloat16),
            pltpu.VMEM((width, SLAB), jnp.float32),
            pltpu.VMEM((width, SLAB), jnp.bfloat16),
            pltpu.SemaphoreType.DMA,
            pltpu.SemaphoreType.DMA((sends,)),
            pltpu.SemaphoreType.DMA((experts, 2)),
            pltpu.SemaphoreType.DMA((width // SLAB,)),
        ],
        compiler_params=pltpu.CompilerParams(
            collective_id=0, has_side_effects=True, vmem_limit_bytes=67043328
        ),
        name="gathered_gram",
    )(bits, own)


def normed_kernel(
    local, partial_ref, residual_ref, gain_ref, out_ref,
    mine, got, mid, far, own_sem, core_send, core_recv, pair_send, pair_recv,
):
    expert, tensor = lax.axis_index("expert"), lax.axis_index("tensor")
    pair, core = lax.div(tensor, 2), lax.rem(tensor, 2)
    other_core = (expert, pair * 2 + 1 - core)
    other_pair = (expert, (1 - pair) * 2 + core)
    parts = 4
    size = local // parts

    def source(p, c, at, count):
        start = pl.multiple_of((p * 2 + c) * local + at, size)
        return partial_ref.at[0, pl.ds(start, count), :]

    loads = []
    for turn, p in enumerate((1 - pair, pair)):
        loads.append(pltpu.make_async_copy(source(p, core, 0, local), mine.at[turn], own_sem.at[turn]))
        loads[-1].start()

    barrier = pltpu.get_barrier_semaphore()
    for peer in (other_core, other_pair):
        pl.semaphore_signal(
            barrier, inc=1, device_id=peer, device_id_type=pl.DeviceIdType.MESH
        )
    pl.semaphore_wait(barrier, 2)

    inside = []
    for turn, p in enumerate((1 - pair, pair)):
        for part in range(parts):
            rows = pl.ds(part * size, size)
            number = turn * parts + part
            inside.append(
                pltpu.make_async_remote_copy(
                    src_ref=source(p, 1 - core, part * size, size),
                    dst_ref=got.at[turn, rows, :],
                    send_sem=core_send.at[number],
                    recv_sem=core_recv.at[number],
                    device_id=other_core,
                    device_id_type=pl.DeviceIdType.MESH,
                )
            )
            inside[-1].start()

    across = []
    loads[0].wait()
    for part in range(parts):
        rows = pl.ds(part * size, size)
        inside[part].wait_recv()
        mid[rows, :] = (
            mine[0, rows, :].astype(jnp.float32) + got[0, rows, :].astype(jnp.float32)
        ).astype(jnp.bfloat16)
        across.append(
            pltpu.make_async_remote_copy(
                src_ref=mid.at[rows, :],
                dst_ref=far.at[rows, :],
                send_sem=pair_send.at[part],
                recv_sem=pair_recv.at[part],
                device_id=other_pair,
                device_id_type=pl.DeviceIdType.MESH,
            )
        )
        if part > 0:
            across[part - 1].start()
    loads[1].wait()
    for part in range(parts):
        inside[parts + part].wait_recv()
    across[parts - 1].start()

    for part in range(parts):
        rows = pl.ds(part * size, size)
        across[part].wait_recv()
        attn = (
            mine[1, rows, :].astype(jnp.float32)
            + got[1, rows, :].astype(jnp.float32)
            + far[rows, :].astype(jnp.float32)
        )
        hidden = residual_ref[rows, :].astype(jnp.float32) + attn
        scale = lax.rsqrt(jnp.mean(hidden * hidden, axis=1, keepdims=True) + 1e-06)
        out_ref[rows, :] = (hidden * scale * gain_ref[...]).astype(jnp.bfloat16)

    for copy in inside + across:
        copy.wait_send()


def normed_rows(attn_partial, residual, norm_gain):
    local, width = residual.shape
    return pl.pallas_call(
        functools.partial(normed_kernel, local),
        out_shape=jax.ShapeDtypeStruct((local, width), jnp.bfloat16),
        in_specs=[
            pl.BlockSpec(memory_space=pl.ANY),
            pl.BlockSpec(memory_space=pltpu.VMEM),
            pl.BlockSpec(memory_space=pltpu.VMEM),
        ],
        out_specs=pl.BlockSpec(memory_space=pltpu.VMEM),
        scratch_shapes=[
            pltpu.VMEM((2, local, width), jnp.bfloat16),
            pltpu.VMEM((2, local, width), jnp.bfloat16),
            pltpu.VMEM((local, width), jnp.bfloat16),
            pltpu.VMEM((local, width), jnp.bfloat16),
            pltpu.SemaphoreType.DMA((2,)),
            pltpu.SemaphoreType.DMA((8,)),
            pltpu.SemaphoreType.DMA((8,)),
            pltpu.SemaphoreType.DMA((4,)),
            pltpu.SemaphoreType.DMA((4,)),
        ],
        compiler_params=pltpu.CompilerParams(collective_id=1, has_side_effects=True),
        name="normed_rows",
    )(attn_partial, residual, norm_gain[None, :])


def rotated_kernel(order_ref, rows_ref, rotation_ref, out_ref, flipped, moved):
    size = rotation_ref.shape[1]
    group = 32

    @pl.loop(0, rotation_ref.shape[0])
    def _(b):
        at = pl.ds(pl.multiple_of(b * size, size), size)
        flipped[at, :] = rows_ref[:, at].astype(jnp.float32).T

    @pl.loop(0, flipped.shape[0] // group)
    def _(step):
        base = pl.multiple_of(step * group, group)
        for j in range(group):
            moved[pl.ds(base + j, 1), :] = flipped[pl.ds(order_ref[base + j], 1), :]

    @pl.loop(0, rotation_ref.shape[0])
    def _(b):
        at = pl.ds(pl.multiple_of(b * size, size), size)
        out_ref[:, at] = lax.dot_general(
            moved[at, :].T.astype(jnp.bfloat16), rotation_ref[b], (((1,), (0,)), ((), ())),
            preferred_element_type=jnp.float32,
        ).astype(jnp.bfloat16)


def rotated_rows(rows, channel_order, rotation):
    local, width = rows.shape
    return pl.pallas_call(
        rotated_kernel,
        out_shape=jax.ShapeDtypeStruct((local, width), jnp.bfloat16),
        in_specs=[
            pl.BlockSpec(memory_space=pltpu.SMEM),
            pl.BlockSpec(memory_space=pltpu.VMEM),
            pl.BlockSpec(memory_space=pltpu.VMEM),
        ],
        out_specs=pl.BlockSpec(memory_space=pltpu.VMEM),
        scratch_shapes=[
            pltpu.VMEM((width, local), jnp.float32),
            pltpu.VMEM((width, local), jnp.float32),
        ],
        name="rotated_rows",
    )(channel_order, rows, rotation)


def on_device(attn_partial, residual, norm_gain, channel_order, rotation, routes, slab_block):
    experts = lax.axis_size("expert") * lax.axis_size("tensor")
    mean_load = residual.shape[0] * routes.shape[1] // experts
    slots = max(2, mean_load + (mean_load + 1) // 2)
    spread_all = residual.shape[0] <= 4 * slots and lax.axis_size("tensor") == 4
    if spread_all:
        normed = normed_rows(attn_partial, residual, norm_gain)
        payload = rotated_rows(normed, channel_order, rotation)
    else:
        summed = lax.psum_scatter(
            attn_partial[0].astype(jnp.float32).astype(jnp.bfloat16),
            "tensor",
            scatter_dimension=0,
            tiled=True,
        ).astype(jnp.float32)
        hidden = residual.astype(jnp.float32) + summed
        scale = lax.rsqrt(jnp.mean(hidden * hidden, axis=1, keepdims=True) + 1e-06)
        normed = (hidden * scale * norm_gain[None, :]).astype(jnp.bfloat16)
        payload = rotate_rows(normed, channel_order, rotation)
    start = slab_block[0] * rotation.shape[1]
    if spread_all:
        return gathered_gram(payload, routes, slab_block, rotation.shape[1])[None]
    rows, count = dispatch_rows(payload, routes)
    slab = lax.dynamic_slice_in_dim(rows, start, SLAB, 1)
    product = lax.dot_general(
        rows, slab, (((0,), (0,)), ((), ())), preferred_element_type=jnp.float32
    )
    return (product * (2.0 / count)).astype(jnp.bfloat16)[None]


def solution(mesh):
    placed = (
        P("tensor", "expert", None),
        P(("expert", "tensor"), None),
        P(),
        P(),
        P(),
        P(("expert", "tensor"), None),
        P(("expert", "tensor")),
    )
    return jax.shard_map(
        on_device,
        mesh=mesh,
        in_specs=placed,
        out_specs=P(("expert", "tensor"), None, None),
        check_vma=False,
    )
```
